32 devices in a mesh: row: 8 (over z, core), col: 4 (over y, x).
Axes of the slice: x: 2, y: 2, z: 4, core: 2. Of those that a mesh axis runs over, the one named last changes fastest.
Arguments:
- shot_traces: float32 [16384, 2, 8192], P(('row', 'col')), may hold values from -0.046875 to 0.046875
- shot_ids: int32 [16384], P(('row', 'col')), may hold values from 0 to 8191, as said below
- shot_counts: int32 [32], P(('row', 'col')), may hold values from 0 to 512, as said below
- missing_blocks: int32 [64, 64], P('row', 'col'), may hold values from 0 to 1, as said below
- weight_bins: int32 [8192], P(('row', 'col')), may hold values from 0 to 63
- weight_table: float32 [64], replicated, may hold values from 0.1 to 1
- focus_panel: float32 [2, 8192, 512], P(None, ('col', 'row')), may hold values from -6 to 6
Outputs:
- wavefield: float32 [2, 8192, 512], P(None, ('row', 'col'))
- adjoint_image: float32 [2, 8192, 512], P(None, ('col', 'row'))
The draws below stay inside these ranges and needn't reach their ends.
Inputs may be any that keep to these rules, and one draw needn't show every extreme that they name: `shot_ids`: over the counted slots of all devices every source appears exactly once; uncounted slots hold arbitrary sources. The counted slots of one device hold at most 64 sources of any block of 1024 consecutive sources, and at most (128) of any block of 2048; some device reaches both. `shot_counts`: some device has all 512 slots counted. `missing_blocks`: diagonal blocks are recorded, and of two mirrored blocks at most one is missing.
All inputs are finite; a program needn't handle non-finite values.
Results may differ from the reference program's by a relative error of at most 0.00007.
Values sent between devices are 32-bit elements; how exact they have to be, the bound alone decides.
A program may use at most 320 MiB of HBM per device.

```python
import math
import jax
import jax.numpy as jnp
from jax import lax

STATIONS = 8192
FOCUS = 512
BLOCK = 128
NBIN = 64
SRC_TILE = 1024
CAP = 64
SLOTS = 512
NBLK = 64
N_ROW = 8
DEVICES = 32


def assign_shots(key):
    base_key = jax.random.fold_in(key, 7)
    keys = jax.random.split(base_key, 5)
    pairing = jax.random.permutation(keys[0], DEVICES).astype(jnp.int32)
    share_first = jax.random.randint(keys[1], (DEVICES // 2, N_ROW), 0, CAP + 1).astype(jnp.int32)
    share_first = share_first.at[0].set(CAP)
    per_block = jnp.zeros((DEVICES, N_ROW), jnp.int32)
    per_block = per_block.at[pairing[0::2]].set(share_first)
    per_block = per_block.at[pairing[1::2]].set(CAP - share_first)
    offsets = jnp.cumsum(per_block, axis=0) - per_block
    orders = jax.vmap(lambda item: jax.random.permutation(item, SRC_TILE))(jax.random.split(keys[2], N_ROW)).astype(jnp.int32)
    within = jnp.arange(CAP, dtype=jnp.int32)
    has_shot = within[None, None, :] < per_block[:, :, None]
    in_block = jnp.where(has_shot, offsets[:, :, None] + within[None, None, :], 0)
    block_rows = jnp.arange(N_ROW, dtype=jnp.int32)[None, :, None]
    sources = block_rows * SRC_TILE + orders[block_rows, in_block]
    slot_start = jnp.cumsum(per_block, axis=1) - per_block
    slot_place = slot_start[:, :, None] + within[None, None, :]
    totals = jnp.sum(per_block, axis=1).astype(jnp.int32)
    scores = jax.random.randint(keys[3], (DEVICES, SLOTS), 0, 1 << 20).astype(jnp.int32) * SLOTS + jnp.arange(SLOTS, dtype=jnp.int32)[None, :]
    is_used = jnp.arange(SLOTS, dtype=jnp.int32)[None, :] < totals[:, None]
    scores = jnp.where(is_used, scores, jnp.int32(2147000000))
    ordering = jnp.argsort(scores, axis=1, stable=True)
    new_place = jnp.argsort(ordering, axis=1, stable=True).astype(jnp.int32)
    device_rows = jnp.broadcast_to(jnp.arange(DEVICES, dtype=jnp.int32)[:, None, None], sources.shape)
    moved = new_place[device_rows, jnp.where(has_shot, slot_place, 0)]
    moved = jnp.where(has_shot, moved, SLOTS)
    filler = jax.random.randint(keys[4], (DEVICES, SLOTS), 0, STATIONS).astype(jnp.int32)
    labels = filler.at[device_rows, moved].set(sources, mode='drop')
    return (labels.reshape(-1), totals)


def draw_shot_ids(key, part):
    return assign_shots(key)[0]


def draw_shot_counts(key, part):
    return assign_shots(key)[1]


def draw_missing_blocks(key, part):
    picks = jax.random.randint(jax.random.fold_in(key, 11), (NBLK, NBLK), 0, 10)
    indices = jnp.arange(NBLK, dtype=jnp.int32)
    above = indices[:, None] < indices[None, :]
    upper_missing = (picks < 2) & above
    lower_missing = (picks >= 2) & (picks < 4) & above
    return (upper_missing | lower_missing.T).astype(jnp.int32)


def place_ends(entries, key, smallest, top_value):
    extent = entries.shape
    index_at = [jax.random.randint(jax.random.fold_in(key, axis), (), 0, extent[axis]) for axis in range(len(extent))]
    entries = entries.at[tuple(index_at)].set(smallest)
    longest = extent.index(max(extent))
    index_at[longest] = (index_at[longest] + 1) % extent[longest]
    return entries.at[tuple(index_at)].set(top_value)


def shard_levels(key, extent, pieces, low, top_value):
    gain, own = 1.0, jax.random.fold_in(key, 6)
    for axis_at, blocks in pieces:
        draws = jnp.exp(jax.random.uniform(jax.random.fold_in(own, axis_at), (blocks,), jnp.float32, low / len(pieces), top_value / len(pieces)))
        gain = gain * jnp.repeat(draws, extent[axis_at] // blocks).reshape([-1 if axis == axis_at else 1 for axis in range(len(extent))])
    return gain


def noise(key, dims, scale, limit, pieces=(), kind=jnp.bfloat16):
    loudness = shard_levels(key, dims, pieces, -0.22, 0.18) if pieces else 1.0
    result = jax.random.normal(key, dims, jnp.float32) * scale * loudness
    return jnp.minimum(jnp.maximum(result, -limit), limit).astype(kind)


def setup_inputs(seed: int = 0) -> dict:
    streams_of = jax.random.split(jax.random.key(seed), 8)
    return {
        "shot_traces": noise(streams_of[0], (DEVICES * SLOTS, 2, STATIONS), (2 * STATIONS) ** -0.5, 0.046875, ((0, 32),), jnp.float32),
        "shot_ids": draw_shot_ids(jax.random.fold_in(streams_of[7], 71), 0),
        "shot_counts": draw_shot_counts(jax.random.fold_in(streams_of[7], 71), 0),
        "missing_blocks": draw_missing_blocks(jax.random.fold_in(streams_of[7], 71), 0),
        "weight_bins": place_ends(jax.random.randint(streams_of[4], (STATIONS,), 0, NBIN), jax.random.fold_in(streams_of[4], 1), 0, NBIN - 1).astype(jnp.int32),
        "weight_table": jnp.clip(jnp.exp(jax.random.uniform(streams_of[5], (NBIN,), jnp.float32, math.log(0.1), math.log(1.0))), 0.1, 1.0),
        "focus_panel": noise(streams_of[6], (2, STATIONS, FOCUS), 1.0, 6.0, ((1, 32),), jnp.float32),
    }


def high_dot(left, right):
    return jnp.dot(left, right, precision=lax.Precision.HIGHEST, preferred_element_type=jnp.float32)


def reference(shot_traces, shot_ids, shot_counts, missing_blocks, weight_bins, weight_table, focus_panel):
    slot_total = shot_traces.shape[0]
    slot_index = jnp.arange(slot_total, dtype=jnp.int32)
    counted = (slot_index % SLOTS) < jnp.repeat(shot_counts, SLOTS)
    target = jnp.where(counted, shot_ids, STATIONS).astype(jnp.int32)
    owner_slot = jnp.zeros((STATIONS,), jnp.int32).at[target].set(slot_index, mode="drop")
    kernel = shot_traces[owner_slot]
    missing_mask = jnp.repeat(jnp.repeat(missing_blocks > 0, BLOCK, axis=0), BLOCK, axis=1)
    kernel_re = jnp.where(missing_mask, kernel[:, 0, :].T, kernel[:, 0, :])
    kernel_im = jnp.where(missing_mask, kernel[:, 1, :].T, kernel[:, 1, :])
    panel_re = focus_panel[0]
    panel_im = focus_panel[1]
    field_re = high_dot(kernel_re, panel_re) - high_dot(kernel_im, panel_im)
    field_im = high_dot(kernel_re, panel_im) + high_dot(kernel_im, panel_re)
    weights = weight_table[weight_bins]
    weighted_re = weights[:, None] * field_re
    weighted_im = weights[:, None] * field_im
    image_re = high_dot(kernel_re.T, weighted_re) + high_dot(kernel_im.T, weighted_im)
    image_im = high_dot(kernel_re.T, weighted_im) - high_dot(kernel_im.T, weighted_re)
    return jnp.stack([field_re, field_im]), jnp.stack([image_re, image_im])
```

```python
import functools

import jax
import jax.numpy as jnp
from jax import lax
from jax.experimental import pallas as pl
from jax.experimental.pallas import tpu as pltpu
from jax.sharding import PartitionSpec as P

AXES = ("row", "col")


def partner(i, j, rows):
    half = rows // 2
    if j:
        return (i + j) % rows
    if i < half:
        return i + half if i % 2 == 0 else i - 1
    return i - half if i % 2 else i + 1


def is_diagonal(i, j, rows):
    return j == 0 and (i % 2 == 1) == (i < rows // 2)


def plan(rows, cols):
    table = [[None] * rows for _ in range(rows)]
    firsts, seconds = [], []
    for i in range(rows):
        for j in range(cols):
            p = i * cols + j
            b = partner(i, j, rows)
            diagonal = is_diagonal(i, j, rows)
            table[i][i if diagonal else b] = 2 * p
            table[b][b if diagonal else i] = 2 * p + 1
            firsts.append(i)
            seconds.append(b)
    total = rows * cols
    assert all(entry is not None for line in table for entry in line)
    to_partner = [(p, seconds[p] * cols + p % cols) for p in range(total)]
    from_partner = [(b, a) for a, b in to_partner]
    to_col_major = [(m, (m % rows) * cols + m // rows) for m in range(total)]
    to_row_major = [(b, a) for a, b in to_col_major]
    return table, firsts, seconds, to_partner, from_partner, to_col_major, to_row_major


def dot(left, right):
    return jnp.dot(left, right, precision=lax.Precision.HIGH, preferred_element_type=jnp.float32)


def trans_dot(left, right):
    return lax.dot_general(
        left,
        right,
        (((0,), (0,)), ((), ())),
        precision=lax.Precision.HIGH,
        preferred_element_type=jnp.float32,
    )


def pack_kernel(table, cap, width, src_ref, x_ref, o_ref, buf, in_sem, out_sem):
    count = len(table)

    def fetch(t):
        s = t % 2

        def one(k, carry):
            pltpu.make_async_copy(
                x_ref.at[src_ref[t * cap + k]], buf.at[s, k], in_sem.at[s]
            ).start()
            return carry

        lax.fori_loop(0, cap, one, 0)

    def outs(t):
        s = t % 2
        return [
            pltpu.make_async_copy(
                buf.at[s, :, :, pl.ds(c * width, width)], o_ref.at[table[t][c]], out_sem.at[s, c]
            )
            for c in range(count)
        ]

    fetch(0)
    for t in range(count):
        s = t % 2
        if t + 1 < count:
            if t >= 1:
                for copy in outs(t - 1):
                    copy.wait()
            fetch(t + 1)
        pltpu.make_async_copy(x_ref.at[pl.ds(0, cap)], buf.at[s], in_sem.at[s]).wait()
        for copy in outs(t):
            copy.start()
    for t in range(max(count - 2, 0), count):
        for copy in outs(t):
            copy.wait()


def pack(traces, source, table, cap, width):
    count = len(table)
    return pl.pallas_call(
        functools.partial(pack_kernel, table, cap, width),
        grid_spec=pltpu.PrefetchScalarGridSpec(
            num_scalar_prefetch=1,
            grid=(1,),
            in_specs=[pl.BlockSpec(memory_space=pl.ANY)],
            out_specs=pl.BlockSpec(memory_space=pl.ANY),
            scratch_shapes=[
                pltpu.VMEM((2, cap, 2, count * width), jnp.float32),
                pltpu.SemaphoreType.DMA((2,)),
                pltpu.SemaphoreType.DMA((2, count)),
            ],
        ),
        out_shape=jax.ShapeDtypeStruct((count * count, cap, 2, width), jnp.float32),
    )(source, traces)


def slot_sources(labels, held_count, group_size, group_count, capacity):
    slot_total = labels.shape[0]
    slot_index = jnp.arange(slot_total, dtype=jnp.int32)
    is_used = slot_index < held_count
    dest_group = labels // group_size
    onehot = (
        (dest_group[:, None] == jnp.arange(group_count, dtype=jnp.int32)[None, :])
        & is_used[:, None]
    ).astype(jnp.int32)
    before = jnp.cumsum(onehot, axis=0) - onehot
    rank_in = jnp.sum(before * onehot, axis=1)
    place = jnp.where(is_used, dest_group * capacity + rank_in, group_count * capacity)
    hit = place[None, :] == jnp.arange(group_count * capacity, dtype=jnp.int32)[:, None]
    source = jnp.sum(jnp.where(hit, slot_index[None, :], 0), axis=1)
    packed_labels = jnp.sum(jnp.where(hit, labels[None, :] + 1, 0), axis=1) - 1
    return source, packed_labels


def row_sources(labels, first_label, length, indices):
    target = jnp.where(labels >= 0, labels - first_label, length)
    return jnp.zeros((length,), jnp.int32).at[target].set(indices, mode="drop")


def lookup(bins, table):
    matches = bins[:, None] == jnp.arange(table.shape[0], dtype=jnp.int32)[None, :]
    return jnp.sum(jnp.where(matches, table[None, :], 0.0), axis=1)


def local(
    shot_traces, shot_ids, shot_counts, missing_blocks, weight_bins, weight_table, focus_panel
):
    slot_total = shot_traces.shape[0]
    stations = shot_traces.shape[2]
    focus = focus_panel.shape[2]
    rows = lax.axis_size("row")
    cols = lax.axis_size("col")
    assert rows == 2 * cols and rows % 4 == 0
    devices = rows * cols
    width = stations // rows
    cap = slot_total // rows
    i = lax.axis_index("row")
    j = lax.axis_index("col")
    me = i * cols + j
    table, firsts, seconds, to_partner, from_partner, to_col_major, to_row_major = plan(rows, cols)
    first = i
    second = jnp.asarray(seconds, jnp.int32)[me]
    diagonals = [is_diagonal(p // cols, p % cols, rows) for p in range(devices)]
    diagonal = jnp.asarray(diagonals, jnp.bool_)[me]
    col_first = jnp.where(diagonal, first, second)
    col_second = jnp.where(diagonal, second, first)

    source, packed_labels = slot_sources(shot_ids, shot_counts[0], width, rows, cap)
    by_group = packed_labels.reshape(rows, cap)
    label_out = jnp.stack(
        [by_group[jnp.asarray(firsts, jnp.int32)], by_group[jnp.asarray(seconds, jnp.int32)]],
        axis=1,
    )
    labels = lax.all_to_all(label_out, AXES, split_axis=0, concat_axis=0, tiled=True)
    packed = pack(shot_traces, source, table, cap, width)
    arrived = lax.all_to_all(
        packed.reshape(devices, 2, cap, 2, width), AXES, split_axis=0, concat_axis=0, tiled=True
    ).reshape(devices * 2 * cap, 2, width)
    indices = jnp.arange(devices * 2 * cap, dtype=jnp.int32).reshape(devices, 2, cap)

    def block(q, group):
        where_from = row_sources(
            labels[:, q].reshape(-1), group * width, width, indices[:, q].reshape(-1)
        )
        taken = jnp.take(arrived, where_from, axis=0, mode="clip")
        return taken[:, 0, :], taken[:, 1, :]

    re0, im0 = block(0, first)
    re1, im1 = block(1, second)

    missing = lax.all_gather(missing_blocks, "row", axis=0, tiled=True)
    missing = lax.all_gather(missing, "col", axis=1, tiled=True)
    blocks = missing.shape[0] // rows
    side = width // blocks

    def mask_of(group, col_group):
        part = lax.dynamic_slice(missing, (group * blocks, col_group * blocks), (blocks, blocks))
        return jnp.broadcast_to(
            part[:, None, :, None] > 0, (blocks, side, blocks, side)
        ).reshape(width, width)

    mask0 = mask_of(first, col_first)
    mask1 = mask_of(second, col_second)

    def fill(mask, own, other):
        return jnp.where(mask, jnp.where(diagonal, own, other).T, own)

    full_re0, full_im0 = fill(mask0, re0, re1), fill(mask0, im0, im1)
    full_re1, full_im1 = fill(mask1, re1, re0), fill(mask1, im1, im0)

    panel = jnp.concatenate([focus_panel[0], focus_panel[1]], axis=1)
    panel = lax.ppermute(panel, AXES, to_row_major)
    panel_first = lax.all_gather(panel, "col", axis=0, tiled=True)
    panel_second = lax.ppermute(panel_first, AXES, from_partner)

    def forward(re, im, vec):
        turned = jnp.concatenate([-vec[:, focus:], vec[:, :focus]], axis=1)
        return dot(re, vec) + dot(im, turned)

    def backward(re, im, vec):
        turned = jnp.concatenate([vec[:, focus:], -vec[:, :focus]], axis=1)
        return trans_dot(re, vec) + trans_dot(im, turned)

    field_second = forward(
        full_re1, full_im1, jnp.where(diagonal, panel_second, panel_first)
    )
    field_moved = lax.ppermute(field_second, AXES, to_partner)
    field_first = forward(full_re0, full_im0, jnp.where(diagonal, panel_first, panel_second))
    own = lax.psum_scatter(field_first + field_moved, "col", scatter_dimension=0, tiled=True)
    weighted = own * lookup(weight_bins, weight_table)[:, None]
    weighted_first = lax.all_gather(weighted, "col", axis=0, tiled=True)
    weighted_second = lax.ppermute(weighted_first, AXES, from_partner)
    image0 = backward(full_re0, full_im0, weighted_first)
    image1 = backward(full_re1, full_im1, weighted_second)
    image_moved = lax.ppermute(jnp.where(diagonal, image1, image0), AXES, to_partner)
    image_sum = jnp.where(diagonal, image0, image1) + image_moved
    image = lax.psum_scatter(image_sum, "col", scatter_dimension=0, tiled=True)
    image = lax.ppermute(image, AXES, to_col_major)
    return (
        jnp.stack([own[:, :focus], own[:, focus:]]),
        jnp.stack([image[:, :focus], image[:, focus:]]),
    )


def solution(mesh):
    placed = (
        P(("row", "col"), None, None),
        P(("row", "col")),
        P(("row", "col")),
        P("row", "col"),
        P(("row", "col")),
        P(),
        P(None, ("col", "row"), None),
    )
    return jax.shard_map(
        local,
        mesh=mesh,
        in_specs=placed,
        out_specs=(P(None, ("row", "col"), None), P(None, ("col", "row"), None)),
        check_vma=False,
    )
```

```python
import functools

import jax
import jax.numpy as jnp
from jax import lax
from jax.experimental import pallas as pl
from jax.experimental.pallas import tpu as pltpu
from jax.sharding import PartitionSpec as P

AXES = ("row", "col")
PIECES = 2


def partner(i, j, rows):
    half = rows // 2
    if j % 2:
        return (i + (j ^ 2 if i % 2 else j)) % rows
    if j:
        return (i + j) % rows
    if i < half:
        return i + half if i % 2 == 0 else i - 1
    return i - half if i % 2 else i + 1


def is_diagonal(i, j, rows):
    return j == 0 and (i % 2 == 1) == (i < rows // 2)


def plan(rows, cols):
    table = [[None] * rows for _ in range(rows)]
    firsts, seconds = [], []
    for i in range(rows):
        for j in range(cols):
            p = i * cols + j
            b = partner(i, j, rows)
            diagonal = is_diagonal(i, j, rows)
            table[i][i if diagonal else b] = 2 * p
            table[b][b if diagonal else i] = 2 * p + 1
            firsts.append(i)
            seconds.append(b)
    total = rows * cols
    assert all(entry is not None for line in table for entry in line)
    to_partner = [(p, seconds[p] * cols + p % cols) for p in range(total)]
    from_partner = [(b, a) for a, b in to_partner]
    to_col_major = [(m, (m % rows) * cols + m // rows) for m in range(total)]
    to_row_major = [(b, a) for a, b in to_col_major]
    return table, firsts, seconds, to_partner, from_partner, to_col_major, to_row_major


def dot(left, right):
    return jnp.dot(left, right, precision=lax.Precision.HIGH, preferred_element_type=jnp.float32)


def trans_dot(left, right):
    return lax.dot_general(
        left,
        right,
        (((0,), (0,)), ((), ())),
        precision=lax.Precision.HIGH,
        preferred_element_type=jnp.float32,
    )


def pack_kernel(table, cap, width, src_ref, x_ref, o_ref, buf, in_sem, out_sem):
    count = len(table)

    def fetch(t):
        s = t % 2

        def one(k, carry):
            pltpu.make_async_copy(
                x_ref.at[src_ref[t * cap + k]], buf.at[s, k], in_sem.at[s]
            ).start()
            return carry

        lax.fori_loop(0, cap, one, 0)

    def outs(t):
        s = t % 2
        return [
            pltpu.make_async_copy(
                buf.at[s, :, :, pl.ds(c * width, width)], o_ref.at[table[t][c]], out_sem.at[s, c]
            )
            for c in range(count)
        ]

    fetch(0)
    for t in range(count):
        s = t % 2
        if t + 1 < count:
            if t >= 1:
                for copy in outs(t - 1):
                    copy.wait()
            fetch(t + 1)
        pltpu.make_async_copy(x_ref.at[pl.ds(0, cap)], buf.at[s], in_sem.at[s]).wait()
        for copy in outs(t):
            copy.start()
    for t in range(max(count - 2, 0), count):
        for copy in outs(t):
            copy.wait()


def pack(traces, source, table, cap, width):
    count = len(table)
    return pl.pallas_call(
        functools.partial(pack_kernel, table, cap, width),
        grid_spec=pltpu.PrefetchScalarGridSpec(
            num_scalar_prefetch=1,
            grid=(1,),
            in_specs=[pl.BlockSpec(memory_space=pl.ANY)],
            out_specs=pl.BlockSpec(memory_space=pl.ANY),
            scratch_shapes=[
                pltpu.VMEM((2, cap, 2, count * width), jnp.float32),
                pltpu.SemaphoreType.DMA((2,)),
                pltpu.SemaphoreType.DMA((2, count)),
            ],
        ),
        out_shape=jax.ShapeDtypeStruct((count * count, cap, 2, width), jnp.float32),
    )(source, traces)


def slot_sources(labels, held_count, group_size, group_count, capacity):
    slot_total = labels.shape[0]
    slot_index = jnp.arange(slot_total, dtype=jnp.int32)
    is_used = slot_index < held_count
    dest_group = labels // group_size
    onehot = (
        (dest_group[:, None] == jnp.arange(group_count, dtype=jnp.int32)[None, :])
        & is_used[:, None]
    ).astype(jnp.int32)
    before = jnp.cumsum(onehot, axis=0) - onehot
    rank_in = jnp.sum(before * onehot, axis=1)
    place = jnp.where(is_used, dest_group * capacity + rank_in, group_count * capacity)
    hit = place[None, :] == jnp.arange(group_count * capacity, dtype=jnp.int32)[:, None]
    source = jnp.sum(jnp.where(hit, slot_index[None, :], 0), axis=1)
    packed_labels = jnp.sum(jnp.where(hit, labels[None, :] + 1, 0), axis=1) - 1
    return source, packed_labels


def row_sources(labels, first_label, length, indices):
    target = jnp.where(labels >= 0, labels - first_label, length)
    return jnp.zeros((length,), jnp.int32).at[target].set(indices, mode="drop")


def lookup(bins, table):
    matches = bins[:, None] == jnp.arange(table.shape[0], dtype=jnp.int32)[None, :]
    return jnp.sum(jnp.where(matches, table[None, :], 0.0), axis=1)


def local(
    shot_traces, shot_ids, shot_counts, missing_blocks, weight_bins, weight_table, focus_panel
):
    slot_total = shot_traces.shape[0]
    stations = shot_traces.shape[2]
    focus = focus_panel.shape[2]
    rows = lax.axis_size("row")
    cols = lax.axis_size("col")
    assert rows == 2 * cols and cols % 4 == 0
    devices = rows * cols
    width = stations // rows
    cap = slot_total // rows
    i = lax.axis_index("row")
    j = lax.axis_index("col")
    me = i * cols + j
    table, firsts, seconds, to_partner, from_partner, to_col_major, to_row_major = plan(rows, cols)
    first = i
    second = jnp.asarray(seconds, jnp.int32)[me]
    diagonals = [is_diagonal(p // cols, p % cols, rows) for p in range(devices)]
    diagonal = jnp.asarray(diagonals, jnp.bool_)[me]
    col_first = jnp.where(diagonal, first, second)
    col_second = jnp.where(diagonal, second, first)

    source, packed_labels = slot_sources(shot_ids, shot_counts[0], width, rows, cap)
    by_group = packed_labels.reshape(rows, cap)
    label_out = jnp.stack(
        [by_group[jnp.asarray(firsts, jnp.int32)], by_group[jnp.asarray(seconds, jnp.int32)]],
        axis=1,
    )
    blocks_down, blocks_across = missing_blocks.shape
    note_size = blocks_down * blocks_across
    panel = jnp.concatenate([focus_panel[0], focus_panel[1]], axis=1)
    panel = lax.ppermute(panel, AXES, to_row_major)
    packed = pack(shot_traces, source, table, cap, width)
    outgoing = jnp.concatenate(
        [
            label_out.reshape(devices, 2 * cap),
            jnp.broadcast_to(missing_blocks.reshape(1, note_size), (devices, note_size)),
        ],
        axis=1,
    )
    packed, outgoing, panel = lax.optimization_barrier((packed, outgoing, panel))
    notes = lax.all_to_all(outgoing, AXES, split_axis=0, concat_axis=0, tiled=True)
    packed, notes = lax.optimization_barrier((packed, notes))
    panel_first = lax.all_gather(panel, "col", axis=0, tiled=True)
    labels = notes[:, : 2 * cap].reshape(devices, 2, cap)
    missing = (
        notes[:, 2 * cap :]
        .reshape(rows, cols, blocks_down, blocks_across)
        .transpose(0, 2, 1, 3)
        .reshape(rows * blocks_down, cols * blocks_across)
    )

    arrived = lax.all_to_all(
        packed.reshape(devices, 2, cap, 2, width), AXES, split_axis=0, concat_axis=0, tiled=True
    )
    arrived, panel_sent = lax.optimization_barrier((arrived, panel_first))
    panel_second = lax.ppermute(panel_sent, AXES, from_partner)
    arrived = arrived.reshape(devices * 2 * cap, 2, width)
    indices = jnp.arange(devices * 2 * cap, dtype=jnp.int32).reshape(devices, 2, cap)

    def block(q, group):
        where_from = row_sources(
            labels[:, q].reshape(-1), group * width, width, indices[:, q].reshape(-1)
        )
        taken = jnp.take(arrived, where_from, axis=0, mode="clip")
        return taken[:, 0, :], taken[:, 1, :]

    re0, im0 = block(0, first)
    re1, im1 = block(1, second)

    blocks = missing.shape[0] // rows
    side = width // blocks

    def mask_of(group, col_group):
        part = lax.dynamic_slice(missing, (group * blocks, col_group * blocks), (blocks, blocks))
        return jnp.broadcast_to(
            part[:, None, :, None] > 0, (blocks, side, blocks, side)
        ).reshape(width, width)

    mask0 = mask_of(first, col_first)
    mask1 = mask_of(second, col_second)

    def fill(mask, own, other):
        return jnp.where(mask, jnp.where(diagonal, own, other).T, own)

    full_re0, full_im0 = fill(mask0, re0, re1), fill(mask0, im0, im1)
    full_re1, full_im1 = fill(mask1, re1, re0), fill(mask1, im1, im0)

    def forward(re, im, vec):
        turned = jnp.concatenate([-vec[:, half:], vec[:, :half]], axis=1)
        return dot(re, vec) + dot(im, turned)

    def backward(re, im, vec):
        turned = jnp.concatenate([vec[:, half:], -vec[:, :half]], axis=1)
        return trans_dot(re, vec) + trans_dot(im, turned)

    def part(vec, h):
        lo = h * half
        return jnp.concatenate([vec[:, lo : lo + half], vec[:, focus + lo : focus + lo + half]], 1)

    half = focus // PIECES
    weights = lookup(weight_bins, weight_table)[:, None]
    vec1 = jnp.where(diagonal, panel_second, panel_first)
    vec0 = jnp.where(diagonal, panel_first, panel_second)
    moved = [
        lax.ppermute(forward(full_re1, full_im1, part(vec1, h)), AXES, to_partner)
        for h in range(PIECES)
    ]
    owns, images = [], []
    for h in range(PIECES):
        field = forward(full_re0, full_im0, part(vec0, h)) + moved[h]
        own = lax.psum_scatter(field, "col", scatter_dimension=0, tiled=True)
        owns.append(own)
        weighted_first = lax.all_gather(own * weights, "col", axis=0, tiled=True)
        weighted_second = lax.ppermute(weighted_first, AXES, from_partner)
        image0 = backward(full_re0, full_im0, weighted_first)
        image1 = backward(full_re1, full_im1, weighted_second)
        image_moved = lax.ppermute(jnp.where(diagonal, image1, image0), AXES, to_partner)
        image = jnp.where(diagonal, image0, image1) + image_moved
        image = lax.psum_scatter(image, "col", scatter_dimension=0, tiled=True)
        images.append(lax.ppermute(image, AXES, to_col_major))

    def join(pieces):
        return jnp.stack(
            [
                jnp.concatenate([piece[:, :half] for piece in pieces], axis=1),
                jnp.concatenate([piece[:, half:] for piece in pieces], axis=1),
            ]
        )

    return join(owns), join(images)


def solution(mesh):
    placed = (
        P(("row", "col"), None, None),
        P(("row", "col")),
        P(("row", "col")),
        P("row", "col"),
        P(("row", "col")),
        P(),
        P(None, ("col", "row"), None),
    )
    return jax.shard_map(
        local,
        mesh=mesh,
        in_specs=placed,
        out_specs=(P(None, ("row", "col"), None), P(None, ("col", "row"), None)),
        check_vma=False,
    )
```
